32 devices in a mesh: group: 2 (over y), gz: 4 (over z), gy: 2 (over x), gx: 2 (over core).
Axes of the slice: x: 2, y: 2, z: 4, core: 2. Of those that a mesh axis runs over, the one named last changes fastest.
Arguments:
- volume: bfloat16 [32, 32, 16, 512], P(None, ('group', 'gz'), 'gy', 'gx'), parts along dimension 1, may hold values from -6 to 6
- first_weight: bfloat16 [3, 3, 3, 32, 32], replicated, may hold values from -0.21875 to 0.21875
- second_weight: bfloat16 [3, 3, 3, 32, 32], replicated, may hold values from -0.21875 to 0.21875
- sample_index: int32 [8, 2, 2, 256], P(('group', 'gz'), 'gy', 'gx'), parts along dimension 0, may hold values from 0 to 8191
- segments: int32 [8, 2, 2, 256], P('group', 'gy', 'gx'), parts along dimension 0, may hold values from 0 to 63
- block_match: int32 [8, 4], P('group'), parts along dimension 0, may hold values from 0 to 1, as said below
Outputs:
- features: bfloat16 [32, 32, 16, 512], P(None, ('group', 'gz'), 'gy', 'gx'), parts along dimension 1
- row_loss: float32 [8, 2, 2, 256], P(('group', 'gz'), 'gy', 'gx'), parts along dimension 0
The draws below stay inside these ranges and needn't reach their ends.
There are 2 independent parts, one for each index of `group`. The reference program is written for one: setup_inputs(seed, part) draws one part's arguments, and reference() takes and returns one part's arrays. A program takes and returns all parts, laid end to end along the dimension named above; an argument that names none is the same for every part. Nothing has to cross between parts.
Inputs may be any that keep to these rules, and one draw needn't show every extreme that they name: `sample_index`: the voxel of a row is z * 8 * 256 + y * 256 + x in its block's local coordinates. `block_match`: entry [a, a2] is 1 when block a contrasts against block a2; the diagonal is 1.
All inputs are finite; a program needn't handle non-finite values.
Results may differ from the reference program's by a relative error of at most 0.0034.
Values may be sent and summed in bfloat16 or wider, within the bound.
A program may use at most 128 MiB of HBM per device.

```python
import jax
import jax.numpy as jnp
from jax import lax

C = 32
CZ = 4
CY = 8
CX = 256
R = 256
NSEG = 64
NZB = 4
NZ = 16
NY = 16
NX = 512
N_GY = 2
N_GX = 2


def draw_block_match(key, part):
    random_bits = jax.random.randint(key, (NZB, NZB), 0, 2)
    diagonal = (jnp.arange(NZB)[:, None] == jnp.arange(NZB)[None, :]).astype(jnp.int32)
    return jnp.maximum(random_bits, diagonal).astype(jnp.int32)


def plant(entries, rng, least, high):
    index_at = [jax.random.randint(jax.random.fold_in(rng, axis), (), 0, length) for axis, length in enumerate(entries.shape)]
    main_axis = entries.shape.index(max(entries.shape))
    next_to = index_at[:main_axis] + [(index_at[main_axis] + 1) % entries.shape[main_axis]] + index_at[main_axis + 1:]
    return entries.at[tuple(index_at)].set(least).at[tuple(next_to)].set(high)


def level_of(key, extent, split, least, high):
    gain = 1.0
    for position, shards_of in split:
        heights = jax.random.uniform(jax.random.fold_in(jax.random.fold_in(key, 6), position), (shards_of,), jnp.float32, least / len(split), high / len(split))
        gain = gain * jnp.repeat(jnp.exp(heights), extent[position] // shards_of).reshape((-1,) + (1,) * (len(extent) - 1 - position))
    return gain


def bell_draw(key, dims, deviation, bound, cuts=(), kind=jnp.bfloat16):
    result = deviation * jax.random.normal(key, dims, jnp.float32)
    if cuts:
        result = result * level_of(key, dims, cuts, -0.22, 0.18)
    return jnp.clip(result, -bound, bound).astype(kind)


def setup_inputs(seed: int = 0, part: int = 0) -> dict:
    splits = jax.random.split(jax.random.key(seed), 7)
    part_keys = jax.random.split(jax.random.fold_in(splits[6], part), 7)
    volume = bell_draw(part_keys[0], (C, NZ, NY, NX), 1.0, 6.0, ((1, 4), (2, 2), (3, 2)))
    first_weight = bell_draw(splits[1], (3, 3, 3, C, C), (27 * C) ** -0.5, 0.21875)
    second_weight = bell_draw(splits[2], (3, 3, 3, C, C), (27 * C) ** -0.5, 0.21875)
    sample_index = plant(jax.random.randint(part_keys[3], (NZB, N_GY, N_GX, R), 0, CZ * CY * CX), jax.random.fold_in(part_keys[3], 1), 0, (CZ * CY * CX) - 1).astype(jnp.int32)
    segments = plant(jax.random.randint(part_keys[4], (NZB, N_GY, N_GX, R), 0, NSEG), jax.random.fold_in(part_keys[4], 1), 0, NSEG - 1).astype(jnp.int32)
    block_match = draw_block_match(jax.random.fold_in(jax.random.fold_in(splits[6], part), 71), part)
    return {"volume": volume, "first_weight": first_weight, "second_weight": second_weight, "sample_index": sample_index, "segments": segments, "block_match": block_match}


SOFTMAX_WARMTH = 0.25

def conv_same(activ_in, weight):
    padded = jnp.pad(activ_in.astype(jnp.float32), ((0, 0), (1, 1), (1, 1), (1, 1)))
    kernel = weight.astype(jnp.float32)
    out_y = activ_in.shape[2]
    out_x = activ_in.shape[3]

    def slab(block_id):
        window = lax.dynamic_slice_in_dim(padded, (block_id * CZ).astype(jnp.int32), CZ + 2, 1)
        reduced_total = jnp.zeros((kernel.shape[3], CZ, out_y, out_x), jnp.float32)
        for offset_z in range(3):
            for offset_y in range(3):
                for column_shift in range(3):
                    reduced_total = reduced_total + jnp.einsum('oi,izyx->ozyx', kernel[offset_z, offset_y, column_shift], window[:, offset_z:offset_z + CZ, offset_y:offset_y + out_y, column_shift:column_shift + out_x])
        return reduced_total
    slabs = lax.map(slab, jnp.arange(NZB, dtype=jnp.int32))
    return jnp.moveaxis(slabs, 0, 1).reshape(kernel.shape[3], NZB * CZ, out_y, out_x)

def reference(volume, first_weight, second_weight, sample_index, segments, block_match):
    hidden = jax.nn.relu(conv_same(volume, first_weight)).astype(jnp.bfloat16)
    features = (conv_same(hidden, second_weight) + volume.astype(jnp.float32)).astype(jnp.bfloat16)
    local_z = sample_index // (CY * CX)
    local_y = sample_index // CX % CY
    local_x = sample_index % CX
    glob_z = local_z + jnp.arange(NZB, dtype=jnp.int32)[:, None, None, None] * CZ
    global_row_coord = local_y + jnp.arange(N_GY, dtype=jnp.int32)[None, :, None, None] * CY
    glob_x = local_x + jnp.arange(N_GX, dtype=jnp.int32)[None, None, :, None] * CX
    picked = features[:, glob_z, global_row_coord, glob_x].astype(jnp.float32)
    embedding = (picked / jnp.sqrt(lax.optimization_barrier(jnp.sum(picked * picked, axis=0)) + 1.0)).astype(jnp.bfloat16)
    tiles = N_GY * N_GX
    emb_cols = jnp.moveaxis(embedding.reshape(embedding.shape[0], NZB, tiles, R), 2, 0)
    seg_cols = jnp.moveaxis(segments.reshape(NZB, tiles, R), 1, 0)
    weights = block_match.astype(jnp.float32)[:, None, :, None]

    def column(pair):
        emb_col, seg_col = pair
        embedding_flat = emb_col.astype(jnp.float32)
        similarity_logits = jnp.einsum('tru,tdk->rudk', embedding_flat, embedding_flat) / SOFTMAX_WARMTH
        exp_terms = jnp.exp(similarity_logits) * weights
        same_seg = (seg_col[:, :, None, None] == seg_col[None, None, :, :]).astype(jnp.float32)
        reduced_total = lax.optimization_barrier(jnp.sum(exp_terms, axis=(2, 3)))
        positive = lax.optimization_barrier(jnp.sum(exp_terms * same_seg, axis=(2, 3)))
        return jnp.log(reduced_total) - jnp.log(positive)
    losses = lax.map(column, (emb_cols, seg_cols))
    row_loss = jnp.moveaxis(losses, 0, 1).reshape(NZB, N_GY, N_GX, R)
    return (features, row_loss)
```

```python
import functools

import jax
import jax.numpy as jnp
from jax import lax
from jax.experimental import pallas as pl
from jax.experimental.pallas import tpu as pltpu
from jax.sharding import PartitionSpec as P

BF = jnp.bfloat16
F32 = jnp.float32
MESH = pl.DeviceIdType.MESH
DIRS = ((1, 0), (-1, 0), (0, 1), (0, -1), (1, 1), (1, -1), (-1, 1), (-1, -1))
NSEG = 64


def iota(shape, dim):
    return lax.broadcasted_iota(jnp.int32, shape, dim)


def mm(a, b):
    return jnp.dot(a, b, preferred_element_type=F32)


def mm_tn(a, b):
    return lax.dot_general(a, b, (((0,), (0,)), ((), ())), preferred_element_type=F32)


def one_hot(mask):
    return jnp.where(mask, 1.0, 0.0).astype(BF)


def kernel(n_gz, n_gy, vol, wt1, wt2, sidx, seg, bm, feat, loss,
           xa, xh, xac, xhc, edge, band, band_halo, emb_all, acc,
           send_sem, recv_sem, xs_sem, xr_sem, es_sem, er_sem):
    gz, gy, gx = lax.axis_index("gz"), lax.axis_index("gy"), lax.axis_index("gx")
    other = 1 - gx

    def inside(dz, dy):
        z, y = gz + dz, gy + dy
        return (z >= 0) & (z < n_gz) & (y >= 0) & (y < n_gy)

    def dev(z, y, x):
        return {"gz": z, "gy": y, "gx": x}

    barrier = pltpu.get_barrier_semaphore()
    count = jnp.int32(n_gz)
    pl.semaphore_signal(barrier, inc=1, device_id=dev(gz, gy, other), device_id_type=MESH)
    for off in range(1, n_gz):
        pl.semaphore_signal(barrier, inc=1, device_id=dev(lax.rem(gz + off, n_gz), gy, gx), device_id_type=MESH)
    for dz, dy in DIRS:
        if dy != 0:
            there = inside(dz, dy)
            count = count + there.astype(jnp.int32)

            @pl.when(there)
            def _():
                pl.semaphore_signal(barrier, inc=1, device_id=dev(gz + dz, gy + dy, gx), device_id_type=MESH)

    def halo_copy(r, d):
        dz, dy = DIRS[d]
        side = slice(0, 32) if dy == 1 else slice(32, 64)
        if dy == 0:
            src = xa.at[r, 4 if dz == 1 else 1]
            dst = xa.at[r, 0 if dz == 1 else 5]
        elif dz == 0:
            src, dst = edge.at[r, :, side, :], xh.at[r, 1:5, side, :]
        else:
            src = edge.at[r, 3 if dz == 1 else 0, side, :]
            dst = xh.at[r, 0 if dz == 1 else 5, side, :]
        return pltpu.make_async_remote_copy(
            src_ref=src, dst_ref=dst, send_sem=send_sem.at[r, d], recv_sem=recv_sem.at[r, d],
            device_id=dev(gz + dz, gy + dy, gx), device_id_type=MESH)

    near = pl.ds(pl.multiple_of(other * 128, 128), 128)

    def x_copy(r, j):
        if j == 3:
            src, dst = xh.at[r, :, :, near], xhc.at[r]
        else:
            planes = (slice(1, 5), slice(0, 1), slice(5, 6))[j]
            src, dst = xa.at[r, planes, :, near], xac.at[r, planes]
        return pltpu.make_async_remote_copy(
            src_ref=src, dst_ref=dst, send_sem=xs_sem.at[r, j], recv_sem=xr_sem.at[r, j],
            device_id=dev(gz, gy, other), device_id_type=MESH)

    def start_round(r):
        for d, (dz, dy) in enumerate(DIRS):
            @pl.when(inside(dz, dy))
            def _():
                halo_copy(r, d).start()
        x_copy(r, 0).start()

    def zero_missing(r):
        for dz, dy in DIRS:
            @pl.when(jnp.logical_not(inside(-dz, -dy)))
            def _():
                side = slice(0, 32) if dy == 1 else slice(32, 64)
                if dy == 0:
                    xa[r, 0 if dz == 1 else 5] = jnp.zeros((256, 256), BF)
                elif dz == 0:
                    xh[r, 1:5, side, :] = jnp.zeros((4, 32, 256), BF)
                else:
                    xh[r, 0 if dz == 1 else 5, side, :] = jnp.zeros((32, 256), BF)

    def finish_round(r):
        for d, (dz, dy) in enumerate(DIRS):
            @pl.when(inside(-dz, -dy))
            def _():
                halo_copy(r, d).wait_recv()
        for j in (1, 2, 3):
            x_copy(r, j).start()
        for j in range(4):
            x_copy(r, j).wait_recv()

    def drain_round(r):
        for d, (dz, dy) in enumerate(DIRS):
            @pl.when(inside(dz, dy))
            def _():
                halo_copy(r, d).wait_send()
        for j in range(4):
            x_copy(r, j).wait_send()

    er, ec = iota((64, 256), 0), iota((64, 256), 1)
    pick_edges = one_hot(ec == jnp.where(er < 32, er * 8 + 7, (er - 32) * 8))

    def keep(r, z, plane):
        xa[r, z + 1] = plane
        edge[r, z] = mm(pick_edges, plane).astype(BF)

    def build(r, wt):
        rows_out = one_hot((iota((256, 32), 0) >> 3) == iota((256, 32), 1))
        spread = one_hot(iota((96, 768), 0) == (iota((96, 768), 1) >> 3))
        hr, hc = iota((96, 192), 0), iota((96, 192), 1)
        home = hr == ((hc >> 6) * 32 + (hc & 31))
        low = one_hot(home & ((hc & 32) == 0))
        high = one_hot(home & ((hc & 32) != 0))
        tap = (iota((256, 768), 1) & 7) - (iota((256, 768), 0) & 7) + 1
        y = iota((256, 192), 0) & 7
        upper = (iota((256, 192), 1) & 32) != 0
        at_edge = y == jnp.where(upper, 7, 0)

        @pl.loop(0, 3)
        def _(c):
            total = jnp.zeros((256, 768), F32)
            for b in range(3):
                wide = mm(wt[c, b], spread).astype(BF)
                total = jnp.where(tap == b, mm(rows_out, wide), total)
            band[r, c] = total.astype(BF)
            ends = (mm(wt[c, 0], low) + mm(wt[c, 2], high)).astype(BF)
            band_halo[r, c] = jnp.where(at_edge, mm(rows_out, ends), 0.0).astype(BF)

    lane = iota((256, 256), 1)
    lane_half = iota((256, 128), 1)
    side_tap = 2 * other

    def conv(r, z):
        main = xa[r, pl.ds(z, 3)].reshape(768, 256)
        halo = xh[r, pl.ds(z, 3)].reshape(192, 256)
        p = [mm(band[r, c], main) + mm(band_halo[r, c], halo) for c in range(3)]
        q = mm(band[r, side_tap], xac[r, pl.ds(z, 3)].reshape(768, 128))
        q = q + mm(band_halo[r, side_tap], xhc[r, pl.ds(z, 3)].reshape(192, 128))
        out = p[1] + jnp.where(lane == 0, 0.0, pltpu.roll(p[0], 1, 1))
        out = out + jnp.where(lane == 255, 0.0, pltpu.roll(p[2], 255, 1))
        first = jnp.where(lane_half == gx - 1, pltpu.roll(q, 1, 1), 0.0)
        last = jnp.where(lane_half == 127 - 128 * gx, pltpu.roll(q, 127, 1), 0.0)
        return out + jnp.concatenate([first, last], axis=1)

    for z in range(4):
        keep(0, z, vol[:, z].astype(F32).reshape(256, 256).astype(BF))
    pl.semaphore_wait(barrier, count)
    start_round(0)
    zero_missing(0)
    zero_missing(1)
    build(0, wt1)
    finish_round(0)

    @pl.loop(0, 4)
    def _(z):
        keep(1, z, jnp.maximum(conv(0, z), 0.0).astype(BF))

    start_round(1)
    build(1, wt2)
    s = sidx[...]
    s_x, s_y, s_z = s & 255, (s >> 8) & 7, s >> 11
    select_x = one_hot(iota((256, 256), 0) == s_x)
    acc[...] = jnp.zeros((256, 256), F32)
    finish_round(1)

    @pl.loop(0, 4)
    def _(z):
        f = (conv(1, z) + xa[0, z + 1].astype(F32)).astype(BF)
        feat[:, z] = f.astype(F32).reshape(32, 8, 256).astype(BF)
        acc[...] = jnp.where(s_z == z, mm(f, select_x), acc[...])

    picked = jnp.where((iota((256, 256), 0) & 7) == s_y, acc[...], 0.0)
    picked = jnp.sum(picked.reshape(32, 8, 256), axis=1)
    norm = jnp.sqrt(jnp.sum(picked * picked, axis=0, keepdims=True) + 1.0)
    emb_all[0] = (picked / norm).astype(BF)

    def emb_copy(off):
        return pltpu.make_async_remote_copy(
            src_ref=emb_all.at[0], dst_ref=emb_all.at[off], send_sem=es_sem.at[off], recv_sem=er_sem.at[off],
            device_id=dev(lax.rem(gz + off, n_gz), gy, gx), device_id_type=MESH)

    for off in range(1, n_gz):
        emb_copy(off).start()
    drain_round(0)
    drain_round(1)
    own = emb_all[0]
    label = iota((NSEG, 256), 0)
    own_seg = one_hot(label == seg[pl.ds(gz, 1), :])
    total = jnp.zeros((1, 256), F32)
    positive = jnp.zeros((1, 256), F32)
    for off in range(n_gz):
        block = lax.rem(gz + n_gz - off, n_gz)
        if off:
            emb_copy(off).wait_recv()
        same = mm_tn(one_hot(label == seg[pl.ds(block, 1), :]), own_seg)
        e = jnp.exp(mm_tn(emb_all[off], own) * 4.0) * bm[gz, block].astype(F32)
        total = total + jnp.sum(e, axis=0, keepdims=True)
        positive = positive + jnp.sum(e * same, axis=0, keepdims=True)
    loss[...] = jnp.log(total) - jnp.log(positive)
    for off in range(1, n_gz):
        emb_copy(off).wait_send()


def by_tap(weight):
    return jnp.transpose(weight, (2, 1, 3, 0, 4)).reshape(3, 3, 32, 96)


def shards(n_gz, n_gy, volume, first_weight, second_weight, sample_index, segments, block_match):
    vmem = pl.BlockSpec(memory_space=pltpu.VMEM)
    dma = pltpu.SemaphoreType.DMA
    features, row_loss = pl.pallas_call(
        functools.partial(kernel, n_gz, n_gy),
        out_shape=(
            jax.ShapeDtypeStruct(volume.shape, BF),
            jax.ShapeDtypeStruct((1, 256), F32),
        ),
        in_specs=[vmem] * 5 + [pl.BlockSpec(memory_space=pltpu.SMEM)],
        out_specs=(vmem, vmem),
        scratch_shapes=[
            pltpu.VMEM((2, 6, 256, 256), BF),
            pltpu.VMEM((2, 6, 64, 256), BF),
            pltpu.VMEM((2, 6, 256, 128), BF),
            pltpu.VMEM((2, 6, 64, 128), BF),
            pltpu.VMEM((2, 4, 64, 256), BF),
            pltpu.VMEM((2, 3, 256, 768), BF),
            pltpu.VMEM((2, 3, 256, 192), BF),
            pltpu.VMEM((n_gz, 32, 256), BF),
            pltpu.VMEM((256, 256), F32),
            dma((2, 8)), dma((2, 8)), dma((2, 4)), dma((2, 4)), dma((n_gz,)), dma((n_gz,)),
        ],
        compiler_params=pltpu.CompilerParams(
            collective_id=0, has_side_effects=True, vmem_limit_bytes=40 << 20),
        name="voxel_contrast",
    )(
        volume, by_tap(first_weight), by_tap(second_weight), sample_index.reshape(1, 256),
        segments.reshape(segments.shape[0], 256), block_match,
    )
    return features, row_loss.reshape(1, 1, 1, 256)


def solution(mesh):
    in_specs = (
        P(None, ("group", "gz"), "gy", "gx"),
        P(),
        P(),
        P(("group", "gz"), "gy", "gx", None),
        P("group", "gy", "gx", None),
        P("group", None),
    )
    out_specs = (P(None, ("group", "gz"), "gy", "gx"), P(("group", "gz"), "gy", "gx", None))
    body = functools.partial(shards, mesh.shape["gz"], mesh.shape["gy"])
    return jax.shard_map(body, mesh=mesh, in_specs=in_specs, out_specs=out_specs, check_vma=False)
```

```python
import functools

import jax
import jax.numpy as jnp
from jax import lax
from jax.experimental import pallas as pl
from jax.experimental.pallas import tpu as pltpu
from jax.sharding import PartitionSpec as P

BF = jnp.bfloat16
F32 = jnp.float32
MESH = pl.DeviceIdType.MESH
DIRS = ((1, 0), (-1, 0), (0, 1), (0, -1), (1, 1), (1, -1), (-1, 1), (-1, -1))
NSEG = 64


def iota(shape, dim):
    return lax.broadcasted_iota(jnp.int32, shape, dim)


def mm(a, b):
    return jnp.dot(a, b, preferred_element_type=F32)


def mm_tn(a, b):
    return lax.dot_general(a, b, (((0,), (0,)), ((), ())), preferred_element_type=F32)


def one_hot(mask):
    return jnp.where(mask, 1.0, 0.0).astype(BF)


def mm_nt(a, b):
    return lax.dot_general(a, b, (((1,), (1,)), ((), ())), preferred_element_type=F32)


def kernel(n_gz, n_gy, vol_hbm, w1_hbm, w2_hbm, sidx_hbm, seg_hbm, bm, feat, loss,
           vol, wts, sidx, seg, xa, xh, xs, xr, q, band, band_halo, part, same, emb_all, acc,
           in_sem, send_sem, recv_sem, xs_sem, xr_sem, es_sem, er_sem):
    gz, gy, gx = lax.axis_index("gz"), lax.axis_index("gy"), lax.axis_index("gx")
    other = 1 - gx

    def inside(dz, dy):
        z, y = gz + dz, gy + dy
        return (z >= 0) & (z < n_gz) & (y >= 0) & (y < n_gy)

    def dev(z, y, x):
        return {"gz": z, "gy": y, "gx": x}

    loads = [
        pltpu.make_async_copy(a, b, in_sem.at[i])
        for i, (a, b) in enumerate((
            (vol_hbm, vol), (w1_hbm, wts.at[0]), (w2_hbm, wts.at[1]), (sidx_hbm, sidx), (seg_hbm, seg)))
    ]
    for load in loads:
        load.start()

    barrier = pltpu.get_barrier_semaphore()
    count = jnp.int32(n_gz)
    pl.semaphore_signal(barrier, inc=1, device_id=dev(gz, gy, other), device_id_type=MESH)
    for off in range(1, n_gz):
        pl.semaphore_signal(barrier, inc=1, device_id=dev(lax.rem(gz + off, n_gz), gy, gx), device_id_type=MESH)
    for dz, dy in DIRS:
        if dy != 0:
            there = inside(dz, dy)
            count = count + there.astype(jnp.int32)

            @pl.when(there)
            def _():
                pl.semaphore_signal(barrier, inc=1, device_id=dev(gz + dz, gy + dy, gx), device_id_type=MESH)

    def target(dz, dy):
        planes = slice(1, 5) if dz == 0 else (slice(0, 1) if dz == 1 else slice(5, 6))
        return planes, slice(0, 32) if dy == 1 else slice(32, 64)

    def halo_copy(r, d):
        dz, dy = DIRS[d]
        to, side = target(dz, dy)
        planes = slice(1, 5) if dz == 0 else (slice(4, 5) if dz == 1 else slice(1, 2))
        if dy == 0:
            src, dst = xa.at[r, planes], xa.at[r, to]
        else:
            src = xa.at[r, planes, slice(224, 256) if dy == 1 else slice(0, 32), :]
            dst = xh.at[r, to, side, :]
        return pltpu.make_async_remote_copy(
            src_ref=src, dst_ref=dst, send_sem=send_sem.at[r, d], recv_sem=recv_sem.at[r, d],
            device_id=dev(gz + dz, gy + dy, gx), device_id_type=MESH)

    def x_copy(r):
        return pltpu.make_async_remote_copy(
            src_ref=xs.at[r], dst_ref=xr.at[r], send_sem=xs_sem.at[r], recv_sem=xr_sem.at[r],
            device_id=dev(gz, gy, other), device_id_type=MESH)

    def picked_dirs(along_z):
        return [(d, dz, dy) for d, (dz, dy) in enumerate(DIRS) if (dz != 0) == along_z]

    def start_halo(r, along_z):
        for d, dz, dy in picked_dirs(along_z):
            @pl.when(inside(dz, dy))
            def _():
                halo_copy(r, d).start()

    def wait_halo(r, along_z):
        for d, dz, dy in picked_dirs(along_z):
            @pl.when(inside(-dz, -dy))
            def _():
                halo_copy(r, d).wait_recv()

    def zero_missing(r):
        for dz, dy in DIRS:
            @pl.when(jnp.logical_not(inside(-dz, -dy)))
            def _():
                to, side = target(dz, dy)
                n = to.stop - to.start
                if dy == 0:
                    xa[r, to] = jnp.zeros((n, 256, 256), BF)
                else:
                    xh[r, to, side, :] = jnp.zeros((n, 32, 256), BF)

    def drain(r):
        for d, (dz, dy) in enumerate(DIRS):
            @pl.when(inside(dz, dy))
            def _():
                halo_copy(r, d).wait_send()
        x_copy(r).wait_send()

    rr, cc = iota((256, 256), 0), iota((256, 256), 1)
    edge_lane = 255 * other

    def build(r):
        place = iota((32, 96), 1) - iota((32, 96), 0)
        wide = jnp.zeros((288, 96), F32)
        for b in range(3):
            wide = wide + mm(wts[r, :, b].reshape(288, 32), one_hot(place == 32 * b))
        wide = wide.astype(BF)
        tap, col = iota((96, 256), 0), iota((96, 256), 1)

        @pl.loop(0, 8)
        def _(y):
            rows = mm(wide, one_hot(tap == col - 32 * y + 32)).astype(BF)
            at = pl.ds(pl.multiple_of(32 * y, 32), 32)
            for a in range(3):
                for c in range(3):
                    n = 32 * (3 * a + c)
                    band[r, c, at, 256 * a:256 * a + 256] = rows[n:n + 32]

        tap, col = iota((96, 192), 0), iota((96, 192), 1)
        low = jnp.zeros((96, 192), F32)
        high = jnp.zeros((96, 192), F32)
        for a in range(3):
            ends = wide[96 * a:96 * a + 96]
            within = (col >> 6) == a
            upper = (col & 32) != 0
            ch = col & 31
            low = low + mm(ends, one_hot(within & jnp.logical_not(upper) & (tap == ch)))
            high = high + mm(ends, one_hot(within & upper & (tap == ch + 64)))
        low, high = low.astype(BF), high.astype(BF)
        for c in range(3):
            band_halo[r, c, 0:32] = low[32 * c:32 * c + 32]
            band_halo[r, c, 32:224] = jnp.zeros((192, 192), BF)
            band_halo[r, c, 224:256] = high[32 * c:32 * c + 32]

    def conv(r, z):
        main = xa[r, pl.ds(z, 3)].reshape(768, 256)
        halo = xh[r, pl.ds(z, 3)].reshape(192, 256)
        p = [mm(band[r, c], main) + mm(band_halo[r, c], halo) for c in range(3)]
        out = p[1] + jnp.where(cc == 0, 0.0, pltpu.roll(p[0], 1, 1))
        part[z] = out + jnp.where(cc == 255, 0.0, pltpu.roll(p[2], 255, 1))

    def send_column(r):
        lanes = iota((16, 256), 1) == edge_lane
        row = iota((16, 256), 0)
        xs[r, :, 0:1536] = mm_nt(one_hot(lanes), xa[r].reshape(1536, 256)).astype(BF)
        ends = jnp.zeros((16, 192), F32)
        for z in range(4):
            ends = ends + mm_nt(one_hot(lanes & (row == z)), xh[r, z:z + 3].reshape(192, 256))
        xs[r, :, 1536:1728] = ends.astype(BF)
        x_copy(r).start()

    def take_column(r):
        x_copy(r).wait_recv()
        row = iota((16, 768), 0)
        col = xr[r, :, 768:1536].astype(F32)
        for z in range(3):
            col = jnp.where(row == z, xr[r, :, 256 * z:256 * z + 768].astype(F32), col)
        side = 2 * other
        q[...] = mm_nt(band[r, side], col.astype(BF)) + mm_nt(band_halo[r, side], xr[r, :, 1536:1728])

    def whole(z):
        col = jnp.sum(jnp.where(iota((256, 16), 1) == z, q[...], 0.0), axis=1, keepdims=True)
        return part[z] + jnp.where(cc == edge_lane, col, 0.0)

    def hide(z):
        xa[1, z + 1] = jnp.maximum(whole(z), 0.0).astype(BF)

    loads[0].wait()
    to_yc = one_hot(cc == (rr & 31) * 8 + (rr >> 5))
    for z in (0, 3, 1, 2):
        xa[0, z + 1] = mm(to_yc, vol[:, z].astype(F32).reshape(256, 256).astype(BF)).astype(BF)
    pl.semaphore_wait(barrier, count)
    start_halo(0, True)
    start_halo(0, False)
    zero_missing(0)
    zero_missing(1)
    for load in loads[1:]:
        load.wait()
    build(0)
    build(1)
    label = iota((NSEG, 256), 0)
    own_seg = one_hot(label == seg[gz])
    for off in range(n_gz):
        block = lax.rem(gz + n_gz - off, n_gz)
        same[off] = mm_tn(one_hot(label == seg[block]), own_seg)
    acc[...] = jnp.zeros((256, 256), F32)
    wait_halo(0, False)
    wait_halo(0, True)
    send_column(0)

    @pl.loop(0, 2)
    def _(i):
        conv(0, 3 * i)

    take_column(0)
    hide(0)
    hide(3)
    start_halo(1, True)

    @pl.loop(1, 3)
    def _(z):
        conv(0, z)
        hide(z)

    start_halo(1, False)
    wait_halo(1, False)

    @pl.loop(1, 3)
    def _(z):
        conv(1, z)

    wait_halo(1, True)
    send_column(1)

    @pl.loop(0, 2)
    def _(i):
        conv(1, 3 * i)

    take_column(1)
    s = sidx[...]
    s_x, s_y, s_z = s & 255, (s >> 8) & 7, s >> 11
    select_x = one_hot(rr == s_x)
    to_cy = one_hot(cc == (rr & 7) * 32 + (rr >> 3))

    @pl.loop(0, 4)
    def _(z):
        f = (whole(z) + xa[0, z + 1].astype(F32)).astype(BF)
        feat[:, z] = mm(to_cy, f).reshape(32, 8, 256).astype(BF)
        acc[...] = jnp.where(s_z == z, mm(f, select_x), acc[...])

    picked = jnp.where((rr >> 5) == s_y, acc[...], 0.0)
    picked = jnp.sum(picked.reshape(8, 32, 256), axis=0)
    norm = jnp.sqrt(jnp.sum(picked * picked, axis=0, keepdims=True) + 1.0)
    emb_all[0] = (picked / norm).astype(BF)

    def emb_copy(off):
        return pltpu.make_async_remote_copy(
            src_ref=emb_all.at[0], dst_ref=emb_all.at[off], send_sem=es_sem.at[off], recv_sem=er_sem.at[off],
            device_id=dev(lax.rem(gz + off, n_gz), gy, gx), device_id_type=MESH)

    for off in range(1, n_gz):
        emb_copy(off).start()
    drain(0)
    drain(1)
    own = emb_all[0]
    total = jnp.zeros((1, 256), F32)
    positive = jnp.zeros((1, 256), F32)
    for off in range(n_gz):
        block = lax.rem(gz + n_gz - off, n_gz)
        if off:
            emb_copy(off).wait_recv()
        e = jnp.exp(mm_tn(emb_all[off], own) * 4.0) * bm[gz, block].astype(F32)
        total = total + jnp.sum(e, axis=0, keepdims=True)
        positive = positive + jnp.sum(e * same[off], axis=0, keepdims=True)
    loss[...] = jnp.log(total) - jnp.log(positive)
    for off in range(1, n_gz):
        emb_copy(off).wait_send()


def shards(n_gz, n_gy, volume, first_weight, second_weight, sample_index, segments, block_match):
    vmem = pl.BlockSpec(memory_space=pltpu.VMEM)
    dma = pltpu.SemaphoreType.DMA
    features, row_loss = pl.pallas_call(
        functools.partial(kernel, n_gz, n_gy),
        out_shape=(
            jax.ShapeDtypeStruct(volume.shape, BF),
            jax.ShapeDtypeStruct((1, 256), F32),
        ),
        in_specs=[pl.BlockSpec(memory_space=pltpu.MemorySpace.HBM)] * 5 + [pl.BlockSpec(memory_space=pltpu.SMEM)],
        out_specs=(vmem, vmem),
        scratch_shapes=[
            pltpu.VMEM(volume.shape, BF),
            pltpu.VMEM((2, 3, 3, 3, 32, 32), BF),
            pltpu.VMEM((1, 256), jnp.int32),
            pltpu.VMEM((n_gz, 1, 256), jnp.int32),
            pltpu.VMEM((2, 6, 256, 256), BF),
            pltpu.VMEM((2, 6, 64, 256), BF),
            pltpu.VMEM((2, 16, 1728), BF),
            pltpu.VMEM((2, 16, 1728), BF),
            pltpu.VMEM((256, 16), F32),
            pltpu.VMEM((2, 3, 256, 768), BF),
            pltpu.VMEM((2, 3, 256, 192), BF),
            pltpu.VMEM((4, 256, 256), F32),
            pltpu.VMEM((n_gz, 256, 256), F32),
            pltpu.VMEM((n_gz, 32, 256), BF),
            pltpu.VMEM((256, 256), F32),
            dma((5,)), dma((2, 8)), dma((2, 8)), dma((2,)), dma((2,)), dma((n_gz,)), dma((n_gz,)),
        ],
        compiler_params=pltpu.CompilerParams(
            collective_id=0, has_side_effects=True, vmem_limit_bytes=40 << 20),
        name="voxel_contrast",
    )(
        volume, first_weight, second_weight, sample_index.reshape(1, 256),
        segments.reshape(segments.shape[0], 1, 256), block_match,
    )
    return features, row_loss.reshape(1, 1, 1, 256)


def solution(mesh):
    in_specs = (
        P(None, ("group", "gz"), "gy", "gx"),
        P(),
        P(),
        P(("group", "gz"), "gy", "gx", None),
        P("group", "gy", "gx", None),
        P("group", None),
    )
    out_specs = (P(None, ("group", "gz"), "gy", "gx"), P(("group", "gz"), "gy", "gx", None))
    body = functools.partial(shards, mesh.shape["gz"], mesh.shape["gy"])
    return jax.shard_map(body, mesh=mesh, in_specs=in_specs, out_specs=out_specs, check_vma=False)
```

```python
import functools

import jax
import jax.numpy as jnp
from jax import lax
from jax.experimental import pallas as pl
from jax.experimental.pallas import tpu as pltpu
from jax.sharding import PartitionSpec as P

BF = jnp.bfloat16
F32 = jnp.float32
MESH = pl.DeviceIdType.MESH
DIRS = ((1, 0), (-1, 0), (0, 1), (0, -1), (1, 1), (1, -1), (-1, 1), (-1, -1))
NSEG = 64


def iota(shape, dim):
    return lax.broadcasted_iota(jnp.int32, shape, dim)


def mm(a, b):
    return jnp.dot(a, b, preferred_element_type=F32)


def mm_tn(a, b):
    return lax.dot_general(a, b, (((0,), (0,)), ((), ())), preferred_element_type=F32)


def one_hot(mask):
    return jnp.where(mask, 1.0, 0.0).astype(BF)


def mm_nt(a, b):
    return lax.dot_general(a, b, (((1,), (1,)), ((), ())), preferred_element_type=F32)


def kernel(n_gz, n_gy, vol_hbm, w1_hbm, w2_hbm, sidx_hbm, seg_hbm, bm, feat, loss,
           vol, wts, sidx, seg, xa, xh, xs, xr, q, band, band_halo, part, same, emb_all, acc,
           in_sem, send_sem, recv_sem, xs_sem, xr_sem, es_sem, er_sem):
    gz, gy, gx = lax.axis_index("gz"), lax.axis_index("gy"), lax.axis_index("gx")
    other = 1 - gx

    def inside(dz, dy):
        z, y = gz + dz, gy + dy
        return (z >= 0) & (z < n_gz) & (y >= 0) & (y < n_gy)

    def dev(z, y, x):
        return {"gz": z, "gy": y, "gx": x}

    loads = [
        pltpu.make_async_copy(a, b, in_sem.at[i])
        for i, (a, b) in enumerate((
            (vol_hbm, vol), (w1_hbm, wts.at[0]), (w2_hbm, wts.at[1]), (sidx_hbm, sidx), (seg_hbm, seg)))
    ]
    for load in loads:
        load.start()

    barrier = pltpu.get_barrier_semaphore()
    count = jnp.int32(n_gz)
    pl.semaphore_signal(barrier, inc=1, device_id=dev(gz, gy, other), device_id_type=MESH)
    for off in range(1, n_gz):
        pl.semaphore_signal(barrier, inc=1, device_id=dev(lax.rem(gz + off, n_gz), gy, gx), device_id_type=MESH)
    for dz, dy in DIRS:
        if dy != 0:
            there = inside(dz, dy)
            count = count + there.astype(jnp.int32)

            @pl.when(there)
            def _():
                pl.semaphore_signal(barrier, inc=1, device_id=dev(gz + dz, gy + dy, gx), device_id_type=MESH)

    def target(dz, dy):
        planes = slice(1, 5) if dz == 0 else (slice(0, 1) if dz == 1 else slice(5, 6))
        return planes, slice(0, 32) if dy == 1 else slice(32, 64)

    def halo_copy(r, d):
        dz, dy = DIRS[d]
        to, side = target(dz, dy)
        planes = slice(1, 5) if dz == 0 else (slice(4, 5) if dz == 1 else slice(1, 2))
        if dy == 0:
            src, dst = xa.at[r, planes], xa.at[r, to]
        else:
            src = xa.at[r, planes, slice(224, 256) if dy == 1 else slice(0, 32), :]
            dst = xh.at[r, to, side, :]
        return pltpu.make_async_remote_copy(
            src_ref=src, dst_ref=dst, send_sem=send_sem.at[r, d], recv_sem=recv_sem.at[r, d],
            device_id=dev(gz + dz, gy + dy, gx), device_id_type=MESH)

    def x_copy(r):
        return pltpu.make_async_remote_copy(
            src_ref=xs.at[r], dst_ref=xr.at[r], send_sem=xs_sem.at[r], recv_sem=xr_sem.at[r],
            device_id=dev(gz, gy, other), device_id_type=MESH)

    def picked_dirs(along_z):
        return [(d, dz, dy) for d, (dz, dy) in enumerate(DIRS) if (dz != 0) == along_z]

    def start_halo(r, along_z):
        for d, dz, dy in picked_dirs(along_z):
            @pl.when(inside(dz, dy))
            def _():
                halo_copy(r, d).start()

    def wait_halo(r, along_z):
        for d, dz, dy in picked_dirs(along_z):
            @pl.when(inside(-dz, -dy))
            def _():
                halo_copy(r, d).wait_recv()

    def zero_missing(r):
        for dz, dy in DIRS:
            @pl.when(jnp.logical_not(inside(-dz, -dy)))
            def _():
                to, side = target(dz, dy)
                n = to.stop - to.start
                if dy == 0:
                    xa[r, to] = jnp.zeros((n, 256, 256), BF)
                else:
                    xh[r, to, side, :] = jnp.zeros((n, 32, 256), BF)

    def drain(r):
        for d, (dz, dy) in enumerate(DIRS):
            @pl.when(inside(dz, dy))
            def _():
                halo_copy(r, d).wait_send()
        x_copy(r).wait_send()

    rr, cc = iota((256, 256), 0), iota((256, 256), 1)
    edge_lane = 255 * other

    def build(r):
        place = iota((32, 96), 1) - iota((32, 96), 0)
        wide = jnp.zeros((288, 96), F32)
        for b in range(3):
            wide = wide + mm(wts[r, :, b].reshape(288, 32), one_hot(place == 32 * b))
        wide = wide.astype(BF)
        tap, col = iota((96, 256), 0), iota((96, 256), 1)

        @pl.loop(0, 8)
        def _(y):
            rows = mm(wide, one_hot(tap == col - 32 * y + 32)).astype(BF)
            at = pl.ds(pl.multiple_of(32 * y, 32), 32)
            for a in range(3):
                for c in range(3):
                    n = 32 * (3 * a + c)
                    band[r, c, at, 256 * a:256 * a + 256] = rows[n:n + 32]

        tap, col = iota((96, 192), 0), iota((96, 192), 1)
        low = jnp.zeros((96, 192), F32)
        high = jnp.zeros((96, 192), F32)
        for a in range(3):
            ends = wide[96 * a:96 * a + 96]
            within = (col >> 6) == a
            upper = (col & 32) != 0
            ch = col & 31
            low = low + mm(ends, one_hot(within & jnp.logical_not(upper) & (tap == ch)))
            high = high + mm(ends, one_hot(within & upper & (tap == ch + 64)))
        low, high = low.astype(BF), high.astype(BF)
        for c in range(3):
            band_halo[r, c, 0:32] = low[32 * c:32 * c + 32]
            band_halo[r, c, 32:224] = jnp.zeros((192, 192), BF)
            band_halo[r, c, 224:256] = high[32 * c:32 * c + 32]

    def conv(r, z):
        main = xa[r, pl.ds(z, 3)].reshape(768, 256)
        halo = xh[r, pl.ds(z, 3)].reshape(192, 256)
        p = [mm(band[r, c], main) + mm(band_halo[r, c], halo) for c in range(3)]
        out = p[1] + jnp.where(cc == 0, 0.0, pltpu.roll(p[0], 1, 1))
        part[z] = out + jnp.where(cc == 255, 0.0, pltpu.roll(p[2], 255, 1))

    def send_column(r):
        lanes = iota((16, 256), 1) == edge_lane
        row = iota((16, 256), 0)
        xs[r, :, 0:1536] = mm_nt(one_hot(lanes), xa[r].reshape(1536, 256)).astype(BF)
        ends = jnp.zeros((16, 192), F32)
        for z in range(4):
            ends = ends + mm_nt(one_hot(lanes & (row == z)), xh[r, z:z + 3].reshape(192, 256))
        xs[r, :, 1536:1728] = ends.astype(BF)
        x_copy(r).start()

    def take_column(r):
        x_copy(r).wait_recv()
        row = iota((16, 768), 0)
        col = xr[r, :, 768:1536].astype(F32)
        for z in range(3):
            col = jnp.where(row == z, xr[r, :, 256 * z:256 * z + 768].astype(F32), col)
        side = 2 * other
        q[...] = mm_nt(band[r, side], col.astype(BF)) + mm_nt(band_halo[r, side], xr[r, :, 1536:1728])

    def whole(z):
        col = jnp.sum(jnp.where(iota((256, 16), 1) == z, q[...], 0.0), axis=1, keepdims=True)
        return part[z] + jnp.where(cc == edge_lane, col, 0.0)

    def hide(z):
        xa[1, z + 1] = jnp.maximum(whole(z), 0.0).astype(BF)

    loads[0].wait()
    to_yc = one_hot(cc == (rr & 31) * 8 + (rr >> 5))
    for z in (0, 3, 1, 2):
        xa[0, z + 1] = mm(to_yc, vol[:, z].astype(F32).reshape(256, 256).astype(BF)).astype(BF)
    pl.semaphore_wait(barrier, count)
    start_halo(0, True)
    start_halo(0, False)
    zero_missing(0)
    zero_missing(1)
    for load in loads[1:]:
        load.wait()
    build(0)
    build(1)
    label = iota((NSEG, 256), 0)
    own_seg = one_hot(label == seg[gz])
    for off in range(n_gz):
        block = lax.rem(gz + n_gz - off, n_gz)
        same[off] = mm_tn(one_hot(label == seg[block]), own_seg)
    acc[...] = jnp.zeros((256, 256), F32)
    wait_halo(0, False)
    wait_halo(0, True)
    send_column(0)

    @pl.loop(0, 2)
    def _(i):
        conv(0, 3 * i)

    take_column(0)
    hide(0)
    hide(3)
    start_halo(1, True)

    @pl.loop(1, 3)
    def _(z):
        conv(0, z)
        hide(z)

    start_halo(1, False)
    wait_halo(1, False)

    @pl.loop(1, 3)
    def _(z):
        conv(1, z)

    wait_halo(1, True)
    send_column(1)

    @pl.loop(0, 2)
    def _(i):
        conv(1, 3 * i)

    take_column(1)
    s = sidx[...]
    s_x, s_y, s_z = s & 255, (s >> 8) & 7, s >> 11
    select_x = one_hot(rr == s_x)
    to_cy = one_hot(cc == (rr & 7) * 32 + (rr >> 3))

    @pl.loop(0, 4)
    def _(z):
        f = (whole(z) + xa[0, z + 1].astype(F32)).astype(BF)
        feat[:, z] = mm(to_cy, f).reshape(32, 8, 256).astype(BF)
        acc[...] = jnp.where(s_z == z, mm(f, select_x), acc[...])

    picked = jnp.where((rr >> 5) == s_y, acc[...], 0.0)
    picked = jnp.sum(picked.reshape(8, 32, 256), axis=0)
    norm = jnp.sqrt(jnp.sum(picked * picked, axis=0, keepdims=True) + 1.0)
    emb_all[0] = (picked / norm).astype(BF)

    def emb_copy(off):
        return pltpu.make_async_remote_copy(
            src_ref=emb_all.at[0], dst_ref=emb_all.at[off], send_sem=es_sem.at[off], recv_sem=er_sem.at[off],
            device_id=dev(lax.rem(gz + off, n_gz), gy, gx), device_id_type=MESH)

    for off in range(1, n_gz):
        emb_copy(off).start()
    drain(0)
    drain(1)
    own = emb_all[0]
    total = jnp.zeros((1, 256), F32)
    positive = jnp.zeros((1, 256), F32)
    for off in range(n_gz):
        block = lax.rem(gz + n_gz - off, n_gz)
        if off:
            emb_copy(off).wait_recv()
        e = jnp.exp(mm_tn(emb_all[off], own) * 4.0) * bm[gz, block].astype(F32)
        total = total + jnp.sum(e, axis=0, keepdims=True)
        positive = positive + jnp.sum(e * same[off], axis=0, keepdims=True)
    loss[...] = jnp.log(total) - jnp.log(positive)
    for off in range(1, n_gz):
        emb_copy(off).wait_send()


def shards(n_gz, n_gy, volume, first_weight, second_weight, sample_index, segments, block_match):
    vmem = pl.BlockSpec(memory_space=pltpu.VMEM)
    dma = pltpu.SemaphoreType.DMA
    features, row_loss = pl.pallas_call(
        functools.partial(kernel, n_gz, n_gy),
        out_shape=(
            jax.ShapeDtypeStruct(volume.shape, BF),
            jax.ShapeDtypeStruct((1, 256), F32),
        ),
        in_specs=[pl.BlockSpec(memory_space=pltpu.MemorySpace.HBM)] * 5 + [pl.BlockSpec(memory_space=pltpu.SMEM)],
        out_specs=(vmem, vmem),
        scratch_shapes=[
            pltpu.VMEM(volume.shape, BF),
            pltpu.VMEM((2, 3, 3, 3, 32, 32), BF),
            pltpu.VMEM((1, 256), jnp.int32),
            pltpu.VMEM((n_gz, 1, 256), jnp.int32),
            pltpu.VMEM((2, 6, 256, 256), BF),
            pltpu.VMEM((2, 6, 64, 256), BF),
            pltpu.VMEM((2, 16, 1728), BF),
            pltpu.VMEM((2, 16, 1728), BF),
            pltpu.VMEM((256, 16), F32),
            pltpu.VMEM((2, 3, 256, 768), BF),
            pltpu.VMEM((2, 3, 256, 192), BF),
            pltpu.VMEM((4, 256, 256), F32),
            pltpu.VMEM((n_gz, 256, 256), F32),
            pltpu.VMEM((n_gz, 32, 256), BF),
            pltpu.VMEM((256, 256), F32),
            dma((5,)), dma((2, 8)), dma((2, 8)), dma((2,)), dma((2,)), dma((n_gz,)), dma((n_gz,)),
        ],
        compiler_params=pltpu.CompilerParams(
            collective_id=0, has_side_effects=True, vmem_limit_bytes=56 << 20),
        name="voxel_contrast",
    )(
        volume, first_weight, second_weight, sample_index.reshape(1, 256),
        segments.reshape(segments.shape[0], 1, 256), block_match,
    )
    return features, row_loss.reshape(1, 1, 1, 256)


def solution(mesh):
    in_specs = (
        P(None, ("group", "gz"), "gy", "gx"),
        P(),
        P(),
        P(("group", "gz"), "gy", "gx", None),
        P("group", "gy", "gx", None),
        P("group", None),
    )
    out_specs = (P(None, ("group", "gz"), "gy", "gx"), P(("group", "gz"), "gy", "gx", None))
    body = functools.partial(shards, mesh.shape["gz"], mesh.shape["gy"])
    return jax.shard_map(body, mesh=mesh, in_specs=in_specs, out_specs=out_specs, check_vma=False)
```

```python
import functools

import jax
import jax.numpy as jnp
from jax import lax
from jax.experimental import pallas as pl
from jax.experimental.pallas import tpu as pltpu
from jax.sharding import PartitionSpec as P

BF = jnp.bfloat16
F32 = jnp.float32
MESH = pl.DeviceIdType.MESH
DIRS = ((1, 0), (-1, 0), (0, 1), (0, -1), (1, 1), (1, -1), (-1, 1), (-1, -1)) + ((1, 0), (-1, 0)) * 3
FACE_ROWS = 64
NSEG = 64


def iota(shape, dim):
    return lax.broadcasted_iota(jnp.int32, shape, dim)


def mm(a, b):
    return jnp.dot(a, b, preferred_element_type=F32)


def mm_tn(a, b):
    return lax.dot_general(a, b, (((0,), (0,)), ((), ())), preferred_element_type=F32)


def one_hot(mask):
    return jnp.where(mask, 1.0, 0.0).astype(BF)


def mm_nt(a, b):
    return lax.dot_general(a, b, (((1,), (1,)), ((), ())), preferred_element_type=F32)


def kernel(n_gz, n_gy, vol_hbm, w1_hbm, w2_hbm, sidx_hbm, seg_hbm, bm_hbm, feat, loss,
           vol, wts, sidx, seg, bm, xa, xh, xs, xr, q, band, band_halo, part, made, same, emb_all, acc,
           in_sem, send_sem, recv_sem, xs_sem, xr_sem, es_sem, er_sem):
    gz, gy, gx = lax.axis_index("gz"), lax.axis_index("gy"), lax.axis_index("gx")
    other = 1 - gx

    def inside(dz, dy):
        z, y = gz + dz, gy + dy
        return (z >= 0) & (z < n_gz) & (y >= 0) & (y < n_gy)

    def dev(z, y, x):
        return {"gz": z, "gy": y, "gx": x}

    loads = [
        pltpu.make_async_copy(a, b, in_sem.at[i])
        for i, (a, b) in enumerate((
            (vol_hbm, vol), (w1_hbm, wts.at[0]), (w2_hbm, wts.at[1]), (sidx_hbm, sidx), (seg_hbm, seg),
            (bm_hbm, bm)))
    ]
    for load in loads:
        load.start()

    barrier = pltpu.get_barrier_semaphore()
    count = jnp.int32(n_gz)
    pl.semaphore_signal(barrier, inc=1, device_id=dev(gz, gy, other), device_id_type=MESH)
    for off in range(1, n_gz):
        pl.semaphore_signal(barrier, inc=1, device_id=dev(lax.rem(gz + off, n_gz), gy, gx), device_id_type=MESH)
    for dz, dy in DIRS:
        if dy != 0:
            there = inside(dz, dy)
            count = count + there.astype(jnp.int32)

            @pl.when(there)
            def _():
                pl.semaphore_signal(barrier, inc=1, device_id=dev(gz + dz, gy + dy, gx), device_id_type=MESH)

    def target(dz, dy):
        planes = slice(1, 5) if dz == 0 else (slice(0, 1) if dz == 1 else slice(5, 6))
        return planes, slice(0, 32) if dy == 1 else slice(32, 64)

    def halo_copy(r, d):
        dz, dy = DIRS[d]
        to, side = target(dz, dy)
        planes = slice(1, 5) if dz == 0 else (slice(4, 5) if dz == 1 else slice(1, 2))
        if dy == 0:
            first = FACE_ROWS * (0 if d < 8 else d // 2 - 3)
            rows = slice(first, first + FACE_ROWS)
            src, dst = xa.at[r, planes, rows, :], xa.at[r, to, rows, :]
        else:
            src = xa.at[r, planes, slice(224, 256) if dy == 1 else slice(0, 32), :]
            dst = xh.at[r, to, side, :]
        return pltpu.make_async_remote_copy(
            src_ref=src, dst_ref=dst, send_sem=send_sem.at[r, d], recv_sem=recv_sem.at[r, d],
            device_id=dev(gz + dz, gy + dy, gx), device_id_type=MESH)

    def x_copy(r):
        return pltpu.make_async_remote_copy(
            src_ref=xs.at[r], dst_ref=xr.at[r], send_sem=xs_sem.at[r], recv_sem=xr_sem.at[r],
            device_id=dev(gz, gy, other), device_id_type=MESH)

    def picked_dirs(along_z):
        return [(d, dz, dy) for d, (dz, dy) in enumerate(DIRS) if (dz != 0) == along_z]

    def start_halo(r, along_z):
        for d, dz, dy in picked_dirs(along_z):
            @pl.when(inside(dz, dy))
            def _():
                halo_copy(r, d).start()

    def wait_halo(r, along_z):
        for d, dz, dy in picked_dirs(along_z):
            @pl.when(inside(-dz, -dy))
            def _():
                halo_copy(r, d).wait_recv()

    def zero_missing(r):
        for dz, dy in DIRS[:8]:
            @pl.when(jnp.logical_not(inside(-dz, -dy)))
            def _():
                to, side = target(dz, dy)
                n = to.stop - to.start
                if dy == 0:
                    xa[r, to] = jnp.zeros((n, 256, 256), BF)
                else:
                    xh[r, to, side, :] = jnp.zeros((n, 32, 256), BF)

    def drain(r):
        for d, (dz, dy) in enumerate(DIRS):
            @pl.when(inside(dz, dy))
            def _():
                halo_copy(r, d).wait_send()
        x_copy(r).wait_send()

    rr, cc = iota((256, 256), 0), iota((256, 256), 1)
    edge_lane = 255 * other

    def build(r):
        place = iota((32, 96), 1) - iota((32, 96), 0)
        wide = jnp.zeros((288, 96), F32)
        for b in range(3):
            wide = wide + mm(wts[r, :, b].reshape(288, 32), one_hot(place == 32 * b))
        wide = wide.astype(BF)
        tap, col = iota((96, 256), 0), iota((96, 256), 1)

        @pl.loop(0, 8)
        def _(y):
            rows = mm(wide, one_hot(tap == col - 32 * y + 32)).astype(BF)
            at = pl.ds(pl.multiple_of(32 * y, 32), 32)
            for a in range(3):
                for c in range(3):
                    n = 32 * (3 * a + c)
                    band[r, c, at, 256 * a:256 * a + 256] = rows[n:n + 32]

        tap, col = iota((96, 192), 0), iota((96, 192), 1)
        low = jnp.zeros((96, 192), F32)
        high = jnp.zeros((96, 192), F32)
        for a in range(3):
            ends = wide[96 * a:96 * a + 96]
            within = (col >> 6) == a
            upper = (col & 32) != 0
            ch = col & 31
            low = low + mm(ends, one_hot(within & jnp.logical_not(upper) & (tap == ch)))
            high = high + mm(ends, one_hot(within & upper & (tap == ch + 64)))
        low, high = low.astype(BF), high.astype(BF)
        for c in range(3):
            band_halo[r, c, 0:32] = low[32 * c:32 * c + 32]
            band_halo[r, c, 32:224] = jnp.zeros((192, 192), BF)
            band_halo[r, c, 224:256] = high[32 * c:32 * c + 32]

    def conv(r, z):
        main = xa[r, pl.ds(z, 3)].reshape(768, 256)
        halo = xh[r, pl.ds(z, 3)].reshape(192, 256)
        p = [mm(band[r, c], main) + mm(band_halo[r, c], halo) for c in range(3)]
        out = p[1] + jnp.where(cc == 0, 0.0, pltpu.roll(p[0], 1, 1))
        part[z] = out + jnp.where(cc == 255, 0.0, pltpu.roll(p[2], 255, 1))

    def send_column(r):
        lanes = iota((16, 256), 1) == edge_lane
        row = iota((16, 256), 0)
        xs[r, :, 0:1536] = mm_nt(one_hot(lanes), xa[r].reshape(1536, 256)).astype(BF)
        ends = jnp.zeros((16, 192), F32)
        for z in range(4):
            ends = ends + mm_nt(one_hot(lanes & (row == z)), xh[r, z:z + 3].reshape(192, 256))
        xs[r, :, 1536:1728] = ends.astype(BF)
        x_copy(r).start()

    def take_column(r):
        x_copy(r).wait_recv()
        row = iota((16, 768), 0)
        col = xr[r, :, 768:1536].astype(F32)
        for z in range(3):
            col = jnp.where(row == z, xr[r, :, 256 * z:256 * z + 768].astype(F32), col)
        side = 2 * other
        q[...] = mm_nt(band[r, side], col.astype(BF)) + mm_nt(band_halo[r, side], xr[r, :, 1536:1728])

    def whole(z):
        col = jnp.sum(jnp.where(iota((256, 16), 1) == z, q[...], 0.0), axis=1, keepdims=True)
        return part[z] + jnp.where(cc == edge_lane, col, 0.0)

    def hide(z):
        xa[1, z + 1] = jnp.maximum(whole(z), 0.0).astype(BF)

    loads[0].wait()
    to_yc = one_hot(cc == (rr & 31) * 8 + (rr >> 5))
    for z in (0, 3, 1, 2):
        xa[0, z + 1] = mm(to_yc, vol[:, z].astype(F32).reshape(256, 256).astype(BF)).astype(BF)
    pl.semaphore_wait(barrier, count)
    start_halo(0, True)
    start_halo(0, False)
    zero_missing(0)
    zero_missing(1)
    for load in loads[1:]:
        load.wait()
    build(0)
    build(1)
    label = iota((NSEG, 256), 0)
    own_seg = one_hot(label == seg[gz])
    for off in range(n_gz):
        block = lax.rem(gz + n_gz - off, n_gz)
        same[off] = mm_tn(one_hot(label == seg[block]), own_seg)
    acc[...] = jnp.zeros((256, 256), F32)
    wait_halo(0, False)
    wait_halo(0, True)
    send_column(0)

    @pl.loop(0, 2)
    def _(i):
        conv(0, 3 * i)

    take_column(0)
    hide(0)
    hide(3)
    start_halo(1, True)

    @pl.loop(1, 3)
    def _(z):
        conv(0, z)
        hide(z)

    start_halo(1, False)
    wait_halo(1, False)

    @pl.loop(1, 3)
    def _(z):
        conv(1, z)

    wait_halo(1, True)
    send_column(1)

    @pl.loop(0, 2)
    def _(i):
        conv(1, 3 * i)

    take_column(1)
    s = sidx[...]
    s_x, s_y, s_z = s & 255, (s >> 8) & 7, s >> 11
    select_x = one_hot(rr == s_x)
    to_cy = one_hot(cc == (rr & 7) * 32 + (rr >> 3))

    @pl.loop(0, 4)
    def _(z):
        f = (whole(z) + xa[0, z + 1].astype(F32)).astype(BF)
        made[z] = f
        acc[...] = jnp.where(s_z == z, mm(f, select_x), acc[...])

    picked = jnp.where((rr >> 5) == s_y, acc[...], 0.0)
    picked = jnp.sum(picked.reshape(8, 32, 256), axis=0)
    norm = jnp.sqrt(jnp.sum(picked * picked, axis=0, keepdims=True) + 1.0)
    emb_all[0] = (picked / norm).astype(BF)

    def emb_copy(off):
        return pltpu.make_async_remote_copy(
            src_ref=emb_all.at[0], dst_ref=emb_all.at[off], send_sem=es_sem.at[off], recv_sem=er_sem.at[off],
            device_id=dev(lax.rem(gz + off, n_gz), gy, gx), device_id_type=MESH)

    for off in range(1, n_gz):
        emb_copy(off).start()

    @pl.loop(0, 4)
    def _(z):
        feat[:, z] = mm(to_cy, made[z]).reshape(32, 8, 256).astype(BF)

    own = emb_all[0]
    total = jnp.zeros((1, 256), F32)
    positive = jnp.zeros((1, 256), F32)
    for off in range(n_gz):
        block = lax.rem(gz + n_gz - off, n_gz)
        if off:
            emb_copy(off).wait_recv()
        e = jnp.exp(mm_tn(emb_all[off], own) * 4.0) * bm[gz, block].astype(F32)
        total = total + jnp.sum(e, axis=0, keepdims=True)
        positive = positive + jnp.sum(e * same[off], axis=0, keepdims=True)
    loss[...] = jnp.log(total) - jnp.log(positive)
    for off in range(1, n_gz):
        emb_copy(off).wait_send()
    drain(0)
    drain(1)


def shards(n_gz, n_gy, volume, first_weight, second_weight, sample_index, segments, block_match):
    vmem = pl.BlockSpec(memory_space=pltpu.VMEM)
    dma = pltpu.SemaphoreType.DMA
    features, row_loss = pl.pallas_call(
        functools.partial(kernel, n_gz, n_gy),
        out_shape=(
            jax.ShapeDtypeStruct(volume.shape, BF),
            jax.ShapeDtypeStruct((1, 256), F32),
        ),
        in_specs=[pl.BlockSpec(memory_space=pltpu.MemorySpace.HBM)] * 6,
        out_specs=(vmem, vmem),
        scratch_shapes=[
            pltpu.VMEM(volume.shape, BF),
            pltpu.VMEM((2, 3, 3, 3, 32, 32), BF),
            pltpu.VMEM((1, 256), jnp.int32),
            pltpu.VMEM((n_gz, 1, 256), jnp.int32),
            pltpu.SMEM(block_match.shape, jnp.int32),
            pltpu.VMEM((2, 6, 256, 256), BF),
            pltpu.VMEM((2, 6, 64, 256), BF),
            pltpu.VMEM((2, 16, 1728), BF),
            pltpu.VMEM((2, 16, 1728), BF),
            pltpu.VMEM((256, 16), F32),
            pltpu.VMEM((2, 3, 256, 768), BF),
            pltpu.VMEM((2, 3, 256, 192), BF),
            pltpu.VMEM((4, 256, 256), F32),
            pltpu.VMEM((4, 256, 256), BF),
            pltpu.VMEM((n_gz, 256, 256), F32),
            pltpu.VMEM((n_gz, 32, 256), BF),
            pltpu.VMEM((256, 256), F32),
            dma((6,)), dma((2, len(DIRS))), dma((2, len(DIRS))), dma((2,)), dma((2,)), dma((n_gz,)), dma((n_gz,)),
        ],
        compiler_params=pltpu.CompilerParams(
            collective_id=0, has_side_effects=True, vmem_limit_bytes=40 << 20),
        name="voxel_contrast",
    )(
        *(pltpu.with_memory_space_constraint(a, pltpu.MemorySpace.HBM) for a in (
            volume, first_weight, second_weight, sample_index.reshape(1, 256),
            segments.reshape(segments.shape[0], 1, 256), block_match)),
    )
    return features, row_loss.reshape(1, 1, 1, 256)


def solution(mesh):
    in_specs = (
        P(None, ("group", "gz"), "gy", "gx"),
        P(),
        P(),
        P(("group", "gz"), "gy", "gx", None),
        P("group", "gy", "gx", None),
        P("group", None),
    )
    out_specs = (P(None, ("group", "gz"), "gy", "gx"), P(("group", "gz"), "gy", "gx", None))
    body = functools.partial(shards, mesh.shape["gz"], mesh.shape["gy"])
    return jax.shard_map(body, mesh=mesh, in_specs=in_specs, out_specs=out_specs, check_vma=False)
```

```python
import functools

import jax
import jax.numpy as jnp
from jax import lax
from jax.experimental import pallas as pl
from jax.experimental.pallas import tpu as pltpu
from jax.sharding import PartitionSpec as P

BF = jnp.bfloat16
F32 = jnp.float32
MESH = pl.DeviceIdType.MESH
DIRS = ((1, 0), (-1, 0), (0, 1), (0, -1), (1, 1), (1, -1), (-1, 1), (-1, -1)) + ((1, 0), (-1, 0)) * 3
FACE_ROWS = 64
NSEG = 64


def iota(shape, dim):
    return lax.broadcasted_iota(jnp.int32, shape, dim)


def mm(a, b):
    return jnp.dot(a, b, preferred_element_type=F32)


def mm_tn(a, b):
    return lax.dot_general(a, b, (((0,), (0,)), ((), ())), preferred_element_type=F32)


def one_hot(mask):
    return jnp.where(mask, 1.0, 0.0).astype(BF)


def mm_nt(a, b):
    return lax.dot_general(a, b, (((1,), (1,)), ((), ())), preferred_element_type=F32)


def kernel(n_gz, n_gy, vol_hbm, w1_hbm, w2_hbm, sidx_hbm, seg_hbm, bm_hbm, feat, loss,
           vol, wts, sidx, seg, bm, xa, xh, xs, xr, q, band, band_halo, part, made, same, emb_all, acc,
           in_sem, send_sem, recv_sem, xs_sem, xr_sem, es_sem, er_sem):
    gz, gy, gx = lax.axis_index("gz"), lax.axis_index("gy"), lax.axis_index("gx")
    other = 1 - gx

    def inside(dz, dy):
        z, y = gz + dz, gy + dy
        return (z >= 0) & (z < n_gz) & (y >= 0) & (y < n_gy)

    def dev(z, y, x):
        return {"gz": z, "gy": y, "gx": x}

    loads = [
        pltpu.make_async_copy(a, b, in_sem.at[i])
        for i, (a, b) in enumerate((
            (vol_hbm, vol), (w1_hbm, wts.at[0]), (w2_hbm, wts.at[1]), (sidx_hbm, sidx), (seg_hbm, seg),
            (bm_hbm, bm)))
    ]
    for load in loads:
        load.start()

    barrier = pltpu.get_barrier_semaphore()
    count = jnp.int32(n_gz)
    pl.semaphore_signal(barrier, inc=1, device_id=dev(gz, gy, other), device_id_type=MESH)
    for off in range(1, n_gz):
        pl.semaphore_signal(barrier, inc=1, device_id=dev(lax.rem(gz + off, n_gz), gy, gx), device_id_type=MESH)
    for dz, dy in DIRS:
        if dy != 0:
            there = inside(dz, dy)
            count = count + there.astype(jnp.int32)

            @pl.when(there)
            def _():
                pl.semaphore_signal(barrier, inc=1, device_id=dev(gz + dz, gy + dy, gx), device_id_type=MESH)

    def target(dz, dy):
        planes = slice(1, 5) if dz == 0 else (slice(0, 1) if dz == 1 else slice(5, 6))
        return planes, slice(0, 32) if dy == 1 else slice(32, 64)

    def halo_copy(r, d):
        dz, dy = DIRS[d]
        to, side = target(dz, dy)
        planes = slice(1, 5) if dz == 0 else (slice(4, 5) if dz == 1 else slice(1, 2))
        if dy == 0:
            first = FACE_ROWS * (0 if d < 8 else d // 2 - 3)
            rows = slice(first, first + FACE_ROWS)
            src, dst = xa.at[r, planes, rows, :], xa.at[r, to, rows, :]
        else:
            src = xa.at[r, planes, slice(224, 256) if dy == 1 else slice(0, 32), :]
            dst = xh.at[r, to, side, :]
        return pltpu.make_async_remote_copy(
            src_ref=src, dst_ref=dst, send_sem=send_sem.at[r, d], recv_sem=recv_sem.at[r, d],
            device_id=dev(gz + dz, gy + dy, gx), device_id_type=MESH)

    def x_copy(r):
        return pltpu.make_async_remote_copy(
            src_ref=xs.at[r], dst_ref=xr.at[r], send_sem=xs_sem.at[r], recv_sem=xr_sem.at[r],
            device_id=dev(gz, gy, other), device_id_type=MESH)

    def picked_dirs(along_z):
        return [(d, dz, dy) for d, (dz, dy) in enumerate(DIRS) if (dz != 0) == along_z]

    def start_halo(r, along_z):
        for d, dz, dy in picked_dirs(along_z):
            @pl.when(inside(dz, dy))
            def _():
                halo_copy(r, d).start()

    def wait_halo(r, along_z):
        for d, dz, dy in picked_dirs(along_z):
            @pl.when(inside(-dz, -dy))
            def _():
                halo_copy(r, d).wait_recv()

    def zero_missing(r):
        for dz, dy in DIRS[:8]:
            @pl.when(jnp.logical_not(inside(-dz, -dy)))
            def _():
                to, side = target(dz, dy)
                n = to.stop - to.start
                if dy == 0:
                    xa[r, to] = jnp.zeros((n, 256, 256), BF)
                else:
                    xh[r, to, side, :] = jnp.zeros((n, 32, 256), BF)

    def drain(r):
        for d, (dz, dy) in enumerate(DIRS):
            @pl.when(inside(dz, dy))
            def _():
                halo_copy(r, d).wait_send()
        x_copy(r).wait_send()

    rr, cc = iota((256, 256), 0), iota((256, 256), 1)
    edge_lane = 255 * other

    def build(r):
        place = iota((32, 96), 1) - iota((32, 96), 0)
        wide = jnp.zeros((288, 96), F32)
        for b in range(3):
            wide = wide + mm(wts[r, :, b].reshape(288, 32), one_hot(place == 32 * b))
        wide = wide.astype(BF)
        tap, col = iota((96, 256), 0), iota((96, 256), 1)

        @pl.loop(0, 8)
        def _(y):
            rows = mm(wide, one_hot(tap == col - 32 * y + 32)).astype(BF)
            at = pl.ds(pl.multiple_of(32 * y, 32), 32)
            for a in range(3):
                for c in range(3):
                    n = 32 * (3 * a + c)
                    band[r, c, at, 256 * a:256 * a + 256] = rows[n:n + 32]

        tap, col = iota((96, 192), 0), iota((96, 192), 1)
        low = jnp.zeros((96, 192), F32)
        high = jnp.zeros((96, 192), F32)
        for a in range(3):
            ends = wide[96 * a:96 * a + 96]
            within = (col >> 6) == a
            upper = (col & 32) != 0
            ch = col & 31
            low = low + mm(ends, one_hot(within & jnp.logical_not(upper) & (tap == ch)))
            high = high + mm(ends, one_hot(within & upper & (tap == ch + 64)))
        low, high = low.astype(BF), high.astype(BF)
        for c in range(3):
            band_halo[r, c, 0:32] = low[32 * c:32 * c + 32]
            band_halo[r, c, 32:224] = jnp.zeros((192, 192), BF)
            band_halo[r, c, 224:256] = high[32 * c:32 * c + 32]

    def conv(r, z):
        main = xa[r, pl.ds(z, 3)].reshape(768, 256)
        halo = xh[r, pl.ds(z, 3)].reshape(192, 256)
        p = [mm(band[r, c], main) + mm(band_halo[r, c], halo) for c in range(3)]
        out = p[1] + jnp.where(cc == 0, 0.0, pltpu.roll(p[0], 1, 1))
        part[z] = out + jnp.where(cc == 255, 0.0, pltpu.roll(p[2], 255, 1))

    def send_column(r):
        lanes = iota((16, 256), 1) == edge_lane
        row = iota((16, 256), 0)
        xs[r, :, 0:1536] = mm_nt(one_hot(lanes), xa[r].reshape(1536, 256)).astype(BF)
        ends = jnp.zeros((16, 192), F32)
        for z in range(4):
            ends = ends + mm_nt(one_hot(lanes & (row == z)), xh[r, z:z + 3].reshape(192, 256))
        xs[r, :, 1536:1728] = ends.astype(BF)
        x_copy(r).start()

    def take_column(r):
        x_copy(r).wait_recv()
        row = iota((16, 768), 0)
        col = xr[r, :, 768:1536].astype(F32)
        for z in range(3):
            col = jnp.where(row == z, xr[r, :, 256 * z:256 * z + 768].astype(F32), col)
        side = 2 * other
        q[...] = mm_nt(band[r, side], col.astype(BF)) + mm_nt(band_halo[r, side], xr[r, :, 1536:1728])

    def whole(z):
        col = jnp.sum(jnp.where(iota((256, 16), 1) == z, q[...], 0.0), axis=1, keepdims=True)
        return part[z] + jnp.where(cc == edge_lane, col, 0.0)

    def hide(z):
        xa[1, z + 1] = jnp.maximum(whole(z), 0.0).astype(BF)

    loads[0].wait()
    to_yc = one_hot(cc == (rr & 31) * 8 + (rr >> 5))
    for z in (0, 3, 1, 2):
        xa[0, z + 1] = mm(to_yc, vol[:, z].astype(F32).reshape(256, 256).astype(BF)).astype(BF)
    pl.semaphore_wait(barrier, count)
    start_halo(0, True)
    start_halo(0, False)
    zero_missing(0)
    zero_missing(1)
    for load in loads[1:]:
        load.wait()
    build(0)
    label = iota((NSEG, 256), 0)
    own_seg = one_hot(label == seg[gz])
    for off in range(n_gz):
        block = lax.rem(gz + n_gz - off, n_gz)
        same[off] = mm_tn(one_hot(label == seg[block]), own_seg)
    acc[...] = jnp.zeros((256, 256), F32)
    wait_halo(0, False)

    @pl.loop(1, 3)
    def _(z):
        conv(0, z)

    wait_halo(0, True)
    send_column(0)

    @pl.loop(0, 2)
    def _(i):
        conv(0, 3 * i)

    take_column(0)
    hide(0)
    hide(3)
    start_halo(1, True)

    hide(1)
    hide(2)
    start_halo(1, False)
    build(1)
    wait_halo(1, False)

    @pl.loop(1, 3)
    def _(z):
        conv(1, z)

    wait_halo(1, True)
    send_column(1)

    @pl.loop(0, 2)
    def _(i):
        conv(1, 3 * i)

    take_column(1)
    s = sidx[...]
    s_x, s_y, s_z = s & 255, (s >> 8) & 7, s >> 11
    select_x = one_hot(rr == s_x)
    to_cy = one_hot(cc == (rr & 7) * 32 + (rr >> 3))

    @pl.loop(0, 4)
    def _(z):
        f = (whole(z) + xa[0, z + 1].astype(F32)).astype(BF)
        made[z] = f
        acc[...] = jnp.where(s_z == z, mm(f, select_x), acc[...])

    picked = jnp.where((rr >> 5) == s_y, acc[...], 0.0)
    picked = jnp.sum(picked.reshape(8, 32, 256), axis=0)
    norm = jnp.sqrt(jnp.sum(picked * picked, axis=0, keepdims=True) + 1.0)
    emb_all[0] = (picked / norm).astype(BF)

    def emb_copy(off):
        return pltpu.make_async_remote_copy(
            src_ref=emb_all.at[0], dst_ref=emb_all.at[off], send_sem=es_sem.at[off], recv_sem=er_sem.at[off],
            device_id=dev(lax.rem(gz + off, n_gz), gy, gx), device_id_type=MESH)

    for off in range(1, n_gz):
        emb_copy(off).start()

    @pl.loop(0, 4)
    def _(z):
        feat[:, z] = mm(to_cy, made[z]).reshape(32, 8, 256).astype(BF)

    own = emb_all[0]
    total = jnp.zeros((1, 256), F32)
    positive = jnp.zeros((1, 256), F32)
    for off in range(n_gz):
        block = lax.rem(gz + n_gz - off, n_gz)
        if off:
            emb_copy(off).wait_recv()
        e = jnp.exp(mm_tn(emb_all[off], own) * 4.0) * bm[gz, block].astype(F32)
        total = total + jnp.sum(e, axis=0, keepdims=True)
        positive = positive + jnp.sum(e * same[off], axis=0, keepdims=True)
    loss[...] = jnp.log(total) - jnp.log(positive)
    for off in range(1, n_gz):
        emb_copy(off).wait_send()
    drain(0)
    drain(1)


def shards(n_gz, n_gy, volume, first_weight, second_weight, sample_index, segments, block_match):
    vmem = pl.BlockSpec(memory_space=pltpu.VMEM)
    dma = pltpu.SemaphoreType.DMA
    features, row_loss = pl.pallas_call(
        functools.partial(kernel, n_gz, n_gy),
        out_shape=(
            jax.ShapeDtypeStruct(volume.shape, BF),
            jax.ShapeDtypeStruct((1, 256), F32),
        ),
        in_specs=[pl.BlockSpec(memory_space=pltpu.MemorySpace.HBM)] * 6,
        out_specs=(vmem, vmem),
        scratch_shapes=[
            pltpu.VMEM(volume.shape, BF),
            pltpu.VMEM((2, 3, 3, 3, 32, 32), BF),
            pltpu.VMEM((1, 256), jnp.int32),
            pltpu.VMEM((n_gz, 1, 256), jnp.int32),
            pltpu.SMEM(block_match.shape, jnp.int32),
            pltpu.VMEM((2, 6, 256, 256), BF),
            pltpu.VMEM((2, 6, 64, 256), BF),
            pltpu.VMEM((2, 16, 1728), BF),
            pltpu.VMEM((2, 16, 1728), BF),
            pltpu.VMEM((256, 16), F32),
            pltpu.VMEM((2, 3, 256, 768), BF),
            pltpu.VMEM((2, 3, 256, 192), BF),
            pltpu.VMEM((4, 256, 256), F32),
            pltpu.VMEM((4, 256, 256), BF),
            pltpu.VMEM((n_gz, 256, 256), F32),
            pltpu.VMEM((n_gz, 32, 256), BF),
            pltpu.VMEM((256, 256), F32),
            dma((6,)), dma((2, len(DIRS))), dma((2, len(DIRS))), dma((2,)), dma((2,)), dma((n_gz,)), dma((n_gz,)),
        ],
        compiler_params=pltpu.CompilerParams(
            collective_id=0, has_side_effects=True, vmem_limit_bytes=40 << 20),
        name="voxel_contrast",
    )(
        *(pltpu.with_memory_space_constraint(a, pltpu.MemorySpace.HBM) for a in (
            volume, first_weight, second_weight, sample_index.reshape(1, 256),
            segments.reshape(segments.shape[0], 1, 256), block_match)),
    )
    return features, row_loss.reshape(1, 1, 1, 256)


def solution(mesh):
    in_specs = (
        P(None, ("group", "gz"), "gy", "gx"),
        P(),
        P(),
        P(("group", "gz"), "gy", "gx", None),
        P("group", "gy", "gx", None),
        P("group", None),
    )
    out_specs = (P(None, ("group", "gz"), "gy", "gx"), P(("group", "gz"), "gy", "gx", None))
    body = functools.partial(shards, mesh.shape["gz"], mesh.shape["gy"])
    return jax.shard_map(body, mesh=mesh, in_specs=in_specs, out_specs=out_specs, check_vma=False)
```
